32 devices in a mesh: groups: 2 (over y), seq: 16 (over z, x, core).
Axes of the slice: x: 2, y: 2, z: 4, core: 2. Of those that a mesh axis runs over, the one named last changes fastest.
Arguments:
- pool_kv: bfloat16 [3072, 1024], P(('groups', 'seq')), parts along dimension 0, may hold values from -6 to 6
- pool_slot: int32 [32], P('groups'), parts along dimension 0, may hold values from 0 to 15, each once
- passage_order: int32 [32], P('groups'), parts along dimension 0, may hold values from 0 to 15, each once
- passage_start: int32 [32], P('groups'), parts along dimension 0, may hold values from 0 to 6784, as said below
- recompute_pos: int32 [32, 56], P('groups'), parts along dimension 0, may hold values from 0 to 383, as said below
- page_table: int32 [3072], P('groups'), parts along dimension 0, may hold values from 0 to 1535, as said below
- fresh_q: bfloat16 [1792, 1024], P(('groups', 'seq')), parts along dimension 0, may hold values from -64 to 64
- fresh_kv: bfloat16 [1792, 256], P(('groups', 'seq')), parts along dimension 0, may hold values from -64 to 64
Outputs:
- attended: bfloat16 [1792, 1024], P(('groups', 'seq')), parts along dimension 0
- decode_cache: bfloat16 [3072, 1024], P(('groups', 'seq')), parts along dimension 0
The draws below stay inside these ranges and needn't reach their ends.
There are 2 independent parts, one for each index of `groups`. The reference program is written for one: setup_inputs(seed, part) draws one part's arguments, and reference() takes and returns one part's arrays. A program takes and returns all parts, laid end to end along the dimension named above; each array names one. Nothing has to cross between parts.
Inputs may be any that keep to these rules, and one draw needn't show every extreme that they name: `passage_start`: increases by at least 384 from one passage to the next; the first is 0 and the last is (15) * 384 + 1024. `recompute_pos`: each row holds 56 different positions of its passage in increasing order. `page_table`: every row of the decode cache receives exactly one page; of the 96 pages of one passage at most 6 go to the 96 rows of one owner, and that many do for some owner.
All inputs are finite; a program needn't handle non-finite values.
Results may differ from the reference program's by a relative error of at most 0.0075.
The reference program's roundings to bfloat16 on the way count: a program that leaves them out, or rounds other values in their place, can miss the bound.
Values may be sent and summed in bfloat16 or wider, within the bound.
A program may use at most 256 MiB of HBM per device.

```python
import jax
import jax.numpy as jnp
from jax import lax

HD = 128
GROUP = 8
TOK_DEV = 384
PAGE = 4
GAP = 1024
PASSAGES = 16
SEL = 56
P_DEV = 96
CONTEXT = 6144


def draw_passage_start(key, part):
    extra = jnp.sort(jax.random.randint(jax.random.fold_in(key, 3), (PASSAGES,), 0, GAP + 1))
    extra = extra.at[0].set(0).at[PASSAGES - 1].set(GAP)
    return (jnp.arange(PASSAGES, dtype=jnp.int32) * TOK_DEV + extra).astype(jnp.int32)


def draw_recompute_pos(key, part):
    row_keys = jax.random.split(jax.random.fold_in(key, 5), PASSAGES)

    def one_row(row_key):
        return jnp.sort(jax.random.permutation(row_key, TOK_DEV)[:SEL])
    return jax.vmap(one_row)(row_keys).astype(jnp.int32)


def draw_page_table(key, part):
    split_keys = jax.random.split(jax.random.fold_in(key, 9), 4)
    owner_map = jax.random.permutation(split_keys[0], PASSAGES)
    device_shift = jax.random.permutation(split_keys[1], PASSAGES)
    spread = max(PASSAGES, P_DEV)
    page_offset = jax.random.permutation(split_keys[2], spread)[:P_DEV] % PASSAGES
    slot_keys = jax.random.split(split_keys[3], PASSAGES)
    slot_order = jax.vmap(lambda slot_key: jax.random.permutation(slot_key, P_DEV))(slot_keys)
    owners = owner_map[(device_shift[:, None] + page_offset[None, :]) % PASSAGES]
    page_slots = slot_order[owners, jnp.arange(P_DEV)[None, :]]
    return (owners * P_DEV + page_slots).reshape(-1).astype(jnp.int32)


def fresh_parts(key):
    split_keys = jax.random.split(jax.random.fold_in(key, 11), 4)
    row_count = PASSAGES * SEL
    query_rows = jnp.clip(jax.random.normal(split_keys[1], (row_count, GROUP * HD)) * 3.0, -20.0, 20.0)
    key_rows = jnp.clip(jax.random.normal(split_keys[2], (row_count, HD)), -6.0, 6.0)
    value_rows = jnp.clip(jax.random.normal(split_keys[3], (row_count, HD)), -6.0, 6.0)
    return (query_rows, jnp.concatenate([key_rows, value_rows], axis=1))


def draw_fresh_q(key, part):
    return fresh_parts(key)[0].astype(jnp.bfloat16)


def draw_fresh_kv(key, part):
    return fresh_parts(key)[1].astype(jnp.bfloat16)


def shard_levels(rng, extent, cuts, smallest, top_value):
    gain, own = 1.0, jax.random.fold_in(rng, 6)
    for axis_at, parts in cuts:
        steps = jnp.exp(jax.random.uniform(jax.random.fold_in(own, axis_at), (parts,), jnp.float32, smallest / len(cuts), top_value / len(cuts)))
        gain = gain * jnp.repeat(steps, extent[axis_at] // parts).reshape([-1 if axis == axis_at else 1 for axis in range(len(extent))])
    return gain


def centred(stream_key, shape, scale, reach, cuts=(), kind=jnp.bfloat16):
    drawn = scale * jax.random.normal(stream_key, shape, jnp.float32)
    if cuts:
        drawn = drawn * shard_levels(stream_key, shape, cuts, -0.22, 0.18)
    return jnp.clip(drawn, -reach, reach).astype(kind)


def setup_inputs(seed: int = 0, part: int = 0) -> dict:
    keys = jax.random.split(jax.random.key(seed), 9)
    part_splits = jax.random.split(jax.random.fold_in(keys[8], part), 9)
    pool_kv = centred(part_splits[0], (PASSAGES * P_DEV, PAGE * 2 * HD), 1.0, 6.0, ((0, 16),))
    pool_slot = jax.random.permutation(part_splits[1], PASSAGES).astype(jnp.int32)
    passage_order = jax.random.permutation(part_splits[2], PASSAGES).astype(jnp.int32)
    passage_start = draw_passage_start(jax.random.fold_in(jax.random.fold_in(keys[8], part), 71), part)
    recompute_pos = draw_recompute_pos(jax.random.fold_in(jax.random.fold_in(keys[8], part), 71), part)
    page_table = draw_page_table(jax.random.fold_in(jax.random.fold_in(keys[8], part), 71), part)
    fresh_q = draw_fresh_q(jax.random.fold_in(jax.random.fold_in(keys[8], part), 71), part)
    fresh_kv = draw_fresh_kv(jax.random.fold_in(jax.random.fold_in(keys[8], part), 71), part)
    return {"pool_kv": pool_kv, "pool_slot": pool_slot, "passage_order": passage_order, "passage_start": passage_start, "recompute_pos": recompute_pos, "page_table": page_table, "fresh_q": fresh_q, "fresh_kv": fresh_kv}


ROPE_BASE = 500000.0


def rotate_pos(vector, positions):
    half_dim = vector.shape[-1] // 2
    frequency = ROPE_BASE ** (-(jnp.arange(half_dim, dtype=jnp.float32) * (2.0 / vector.shape[-1])))
    angles = positions.astype(jnp.float32)[..., None] * frequency
    cosine = jnp.cos(angles)
    sine = jnp.sin(angles)
    lower_half = vector[..., :half_dim]
    upper_half = vector[..., half_dim:]
    return jnp.concatenate([lower_half * cosine - upper_half * sine, upper_half * cosine + lower_half * sine], axis=-1)


def reference(pool_kv, pool_slot, passage_order, passage_start, recompute_pos, page_table, fresh_q, fresh_kv):
    page_ids = jnp.arange(P_DEV, dtype=jnp.int32)
    passage_ids = jnp.arange(PASSAGES, dtype=jnp.int32)
    spot_index = pool_slot[passage_order][:, None] * P_DEV + page_ids[None, :]
    pool_rows = (spot_index % PASSAGES) * P_DEV + spot_index // PASSAGES
    cached = pool_kv[pool_rows.reshape(-1)].reshape(PASSAGES, TOK_DEV, 2, HD)
    start_grid = jnp.broadcast_to(passage_start[:, None], (PASSAGES, TOK_DEV))
    shifted = rotate_pos(cached[:, :, 0, :].astype(jnp.float32), start_grid)
    fresh_rows = fresh_kv.reshape(PASSAGES, SEL, 2 * HD)
    fresh_pos = passage_start[:, None] + recompute_pos
    fresh_keys = rotate_pos(fresh_rows[:, :, :HD].astype(jnp.float32), fresh_pos)
    passage_grid = jnp.broadcast_to(passage_ids[:, None], (PASSAGES, SEL))
    key_rows = shifted.at[passage_grid, recompute_pos].set(fresh_keys).astype(jnp.bfloat16)
    value_rows = cached[:, :, 1, :].at[passage_grid, recompute_pos].set(fresh_rows[:, :, HD:])
    page_rows = jnp.stack([key_rows, value_rows], axis=2).reshape(PASSAGES * P_DEV, PAGE * 2 * HD)
    decode_cache = jnp.zeros_like(page_rows).at[page_table].set(page_rows)
    queries = rotate_pos(fresh_q.reshape(PASSAGES, SEL, GROUP, HD).astype(jnp.float32), fresh_pos[:, :, None]).astype(jnp.bfloat16)
    flat_keys = key_rows.reshape(CONTEXT, HD)
    flat_values = value_rows.reshape(CONTEXT, HD)
    key_index = jnp.arange(CONTEXT, dtype=jnp.int32)
    query_places = passage_ids[:, None] * TOK_DEV + recompute_pos

    def attend_passage(inputs):
        query_rows, query_place = inputs
        flat_queries = query_rows.reshape(SEL * GROUP, HD)
        limit = jnp.repeat(query_place, GROUP)
        scores = jnp.dot(flat_queries, flat_keys.T, preferred_element_type=jnp.float32) * (HD ** -0.5)
        allowed = key_index[None, :] <= limit[:, None]
        peak_score = jnp.max(jnp.where(allowed, scores, -jnp.inf), axis=1, keepdims=True)
        weights = jnp.where(allowed, jnp.exp(scores - peak_score), 0.0)
        weight_sum = jnp.sum(weights, axis=1, keepdims=True)
        mixed = jnp.dot(weights.astype(jnp.bfloat16), flat_values, preferred_element_type=jnp.float32) / weight_sum
        return mixed.astype(jnp.bfloat16).reshape(SEL, GROUP * HD)

    attended = lax.map(attend_passage, (queries, query_places)).reshape(PASSAGES * SEL, GROUP * HD)
    return attended, decode_cache
```

```python
import jax
import jax.numpy as jnp
from jax import lax
from jax.experimental import pallas as pl
from jax.experimental.pallas import tpu as pltpu
from jax.sharding import PartitionSpec as P

GROUP = 8
PAGE = 4
ROPE_BASE = 500000.0
LOG2_E = 1.4426950408889634
FAR = 2**30
LOW = -1e30
MESH = pl.DeviceIdType.MESH
FRESH = -1


def pool_parts(rows, count):
    halves = max(2, 2 * (count // 4 - 1))
    half = rows // 2
    cut = max(half, rows * (halves - 1) // halves // 16 * 16)
    lined = [(0, half), (half, cut - half)] if cut > half else [(0, half)]
    return half, lined, (cut, rows - cut)


def iota(shape, dim):
    return lax.broadcasted_iota(jnp.int32, shape, dim)


def divide(number, by):
    return jnp.floor((number.astype(jnp.float32) + 0.5) * (1.0 / by)).astype(jnp.int32)


def total(array, dim):
    return jnp.sum(array, axis=dim, keepdims=True)


def column(row):
    size = row.shape[1]
    same = iota((size, size), 0) == iota((size, size), 1)
    return total(jnp.where(same, jnp.broadcast_to(row, (size, size)), 0), 1)


def split(positions):
    low = positions & 3
    return tuple(
        part.astype(jnp.float32).astype(jnp.bfloat16) for part in (positions - low, low)
    )


def angles(positions, frequency):
    angle = positions.astype(jnp.float32) * frequency
    sine = jnp.sin(angle)
    lower = iota(angle.shape, 1) < angle.shape[1] // 2
    return jnp.cos(angle), jnp.where(lower, -sine, sine)


def turn(vector, cosine, sine):
    return vector * cosine + pltpu.roll(vector, vector.shape[1] // 2, 1) * sine


def dot(left, right):
    return jnp.dot(left, right, preferred_element_type=jnp.float32)


def dot_nt(left, right):
    return lax.dot_general(
        left, right, (((1,), (1,)), ((), ())), preferred_element_type=jnp.float32
    )


def kernel(
    count, pool, *refs,
):
    inputs, refs = refs[:8], refs[8:]
    (attended, pages), refs = refs[:2], refs[2:]
    pool_all, fresh_all, refs = refs[0], refs[1], refs[2:]
    held, refs = refs[:8], refs[8:]
    fresh_kv, fresh_q, slot_ref, order_ref, start_ref, recompute_ref, table_ref, freq_ref = held
    (
        query_ref, limit_ref, cos_ref, sin_ref, key_pos, page_pos, fresh_pos, wanted_ref, keep_ref,
        peak_ref, mixed_ref, page_acc, fresh_acc, send_sem, recv_sem, local_sem,
    ) = refs

    page_count = pool.shape[0]
    tokens = page_count * PAGE
    width = fresh_kv.shape[1]
    dim = width // 2
    sel = fresh_kv.shape[0]
    length = count // 4
    half, lined_pool, last_pool = pool_parts(page_count, count)
    parts = [lined_pool[0], FRESH, *lined_pool[1:], last_pool]
    last = len(parts) - 1
    fresh = 1
    lined = range(last)
    pool_lined = [part for part in lined if part != fresh]
    shared = page_count % count == 0

    me = lax.axis_index("seq")
    at = me // 4
    inner = lax.rem(me, 4)
    core = lax.rem(inner, 2)
    across_inner = lax.rem(inner + 2, 4)
    across = at * 4 + across_inner
    sibling = me + 1 - 2 * core
    twin_inner = inner + 1 - 2 * core
    across_twin = lax.rem(twin_inner + 2, 4)
    up, down = me + 4, me - 4
    has_up, has_down = at < length - 1, at > 0

    barrier = pltpu.get_barrier_semaphore()

    def greet(device):
        pl.semaphore_signal(barrier, inc=1, device_id={"seq": device}, device_id_type=MESH)

    greet(across)
    greet(sibling)
    pl.when(has_up)(lambda: greet(up))
    pl.when(has_down)(lambda: greet(down))

    local = [
        pltpu.make_async_copy(source, target, local_sem.at[at_])
        for at_, (source, target) in enumerate(zip(inputs, held))
    ]
    own_copy = pltpu.make_async_copy(pool, pool_all.at[me], local_sem.at[len(local)])
    for one in local:
        one.start()
    own_copy.start()

    pl.semaphore_wait(barrier, 2 + jnp.where(has_up, 1, 0) + jnp.where(has_down, 1, 0))

    def copy(part, block, way, device, own=False):
        if parts[part] == FRESH:
            source = target = fresh_all.at[block]
        else:
            rows = pl.ds(*parts[part])
            target = pool_all.at[block, rows]
            source = pool.at[rows] if own else target
        return pltpu.make_async_remote_copy(
            src_ref=source,
            dst_ref=target,
            send_sem=send_sem.at[way, part, block],
            recv_sem=recv_sem.at[part, block],
            device_id={"seq": device},
            device_id_type=MESH,
        )

    def begin(part, block, way, device, own=False):
        copy(part, block, way, device, own).start()

    def settle(part, block, way, device, own=False):
        copy(part, block, way, device, own).wait_send()

    def arrive(part, block):
        copy(part, block, 0, sibling).wait_recv()

    def send_lined(act, part):
        pl.when(has_up)(lambda: act(part, me, 0, up, True))
        pl.when(has_down)(lambda: act(part, me, 1, down, True))

    def send_pool(act):
        act(last, me, 2, across, True)
        for part in (*pool_lined, last):
            send_lined(act, part)
        for part in pool_lined:
            act(part, me, 2, across, True)
        for part in (last, *pool_lined):
            act(part, me, 3, sibling, True)

    def send_fresh(act):
        send_lined(act, fresh)
        act(fresh, me, 2, across, True)
        act(fresh, me, 3, sibling, True)

    def pass_across_first(act):
        pl.when(has_up)(lambda: act(last, across, 0, up))
        pl.when(has_down)(lambda: act(last, across, 1, down))
        act(last, across, 3, sibling)

    def line(step, part, act, wait):
        for where in (inner,) if part != last else (inner, across_inner):
            for way, exists, more, device, place in (
                (0, at - step >= 0, has_up, up, at - step),
                (1, at + step < length, has_down, down, at + step),
            ):
                block = place * 4 + where

                @pl.when(exists)
                def _(block=block, way=way, more=more, device=device):
                    if wait:
                        arrive(part, block)
                    pl.when(more)(lambda: act(part, block, way, device))
                    if part != last:
                        act(part, block, 2, across)
                    act(part, block, 3, sibling)

    def crossed(step, part, act, wait):
        for exists, place in (
            (at - step >= 0, at - step),
            ((at + step < length) & (step > 0), at + step),
        ):

            @pl.when(exists)
            def _(place=place):
                block = place * 4 + across_inner
                if wait:
                    arrive(part, block)
                act(part, block, 3, sibling)

    send_pool(begin)

    for one in local:
        one.wait()

    frequency = freq_ref[...]
    lane_mine = iota((1, count), 1) == me
    my_start = total(jnp.where(lane_mine, start_ref[...], 0), 1)
    picked = column(recompute_ref[pl.ds(me, 1), :])
    cosine, sine = angles(my_start + picked, frequency)
    raw = fresh_kv[...]
    turned = turn(raw[:, :dim].astype(jnp.float32), cosine, sine)
    fresh_all[me] = jnp.concatenate(
        [turned, raw[:, dim:].astype(jnp.float32)], axis=1
    ).astype(jnp.bfloat16)

    query_ref[...] = jnp.concatenate(
        [
            turn(fresh_q[:, head * dim : (head + 1) * dim].astype(jnp.float32), cosine, sine)
            for head in range(GROUP)
        ],
        axis=0,
    ).astype(jnp.bfloat16)
    limit_ref[...] = jnp.concatenate([me * tokens + picked] * GROUP, axis=0)
    send_fresh(begin)

    arrive(last, across)
    pass_across_first(begin)

    order = column(order_ref[...])
    slots = total(jnp.where(order == iota((count, count), 1), slot_ref[...], 0), 1)
    square = (count, count)
    slots_row = total(
        jnp.where(iota(square, 0) == iota(square, 1), jnp.broadcast_to(slots, square), 0), 0
    )

    def turn_table(place, block):
        spot = iota((page_count, 1), 0) * count + block
        mine = divide(spot, page_count) == slots_row
        cosine, sine = angles(total(jnp.where(mine, start_ref[...], 0), 1), frequency)
        cos_ref[place] = cosine
        sin_ref[place] = sine

    if shared:
        turn_table(0, 0)
    else:

        @pl.loop(0, count)
        def _(block):
            turn_table(block, block)

    recompute = recompute_ref[...]
    high, low = split(recompute)
    eye = jnp.where(iota((sel, sel), 0) == iota((sel, sel), 1), 1.0, 0.0).astype(jnp.bfloat16)
    high_t = dot_nt(eye, high).astype(jnp.bfloat16)
    low_t = dot_nt(eye, low).astype(jnp.bfloat16)

    def locate(place, first, size):
        lane = iota((1, size), 1)
        token = divide(lane, 4 * half)
        lane = lane - token * (4 * half)
        which = divide(lane, half)
        spot = (lane - which * half + first) * count + place * 4 + which
        slot = divide(spot, page_count)
        page = spot - slot * page_count
        hot = slots == slot
        passage = total(jnp.where(hot, iota((count, size), 0), 0), 0)
        return token, page, passage, hot

    @pl.loop(0, length)
    def _(place):
        for unit in range(2):
            token, page, passage, hot = locate(place, unit * half, PAGE * 4 * half)
            hot = jnp.where(hot, 1.0, 0.0).astype(jnp.bfloat16)
            known = dot(high_t, hot) + dot(low_t, hot)
            spot = page * PAGE + token
            replaced = jnp.max(
                jnp.where(known == spot.astype(jnp.float32), 1, 0), axis=0, keepdims=True
            )
            key_pos[place * 2 + unit] = jnp.where(replaced > 0, FAR, passage * tokens + spot)
            token, page, passage, hot = locate(place, unit * half, 4 * half)
            page_pos[place * 2 + unit] = passage * page_count + page

    many = 4 * sel
    lane = iota((1, many), 1)
    which = divide(lane, sel)
    spread = jnp.where(iota((sel, many), 0) == lane - which * sel, 1.0, 0.0).astype(jnp.bfloat16)
    spread = (dot(high, spread) + dot(low, spread)).astype(jnp.int32)
    spread = spread + iota((count, many), 0) * tokens

    @pl.loop(0, length)
    def _(place):
        chosen = iota((count, many), 0) == place * 4 + which
        fresh_pos[place] = total(jnp.where(chosen, spread, 0), 0)

    row_ids = me * page_count + iota((page_count, 1), 0)
    lanes = table_ref.shape[1]

    def find(at_, wanted):
        match = table_ref[pl.ds(at_, 1), :] == row_ids
        return wanted + jnp.where(match, at_ * lanes + iota((page_count, lanes), 1), 0)

    wanted = lax.fori_loop(
        0, table_ref.shape[0], find, jnp.zeros((page_count, lanes), jnp.int32)
    )
    wanted = total(wanted, 1)
    wanted_ref[...] = wanted
    from_passage = divide(wanted, page_count)
    hot = jnp.where(from_passage == iota((page_count, count), 1), 1.0, 0.0).astype(jnp.bfloat16)
    known = dot(hot, high) + dot(hot, low)
    for token in range(PAGE):
        spot = (wanted - from_passage * page_count) * PAGE + token
        replaced = jnp.max(
            jnp.where(known == spot.astype(jnp.float32), 1.0, 0.0), axis=1, keepdims=True
        )
        keep_ref[token] = 1.0 - replaced

    peak_ref[...] = jnp.full(peak_ref.shape, LOW, jnp.float32)
    mixed_ref[...] = jnp.zeros(mixed_ref.shape, jnp.float32)
    page_acc[...] = jnp.zeros(page_acc.shape, jnp.float32)
    fresh_acc[...] = jnp.zeros(fresh_acc.shape, jnp.float32)
    slope = dim ** (-0.5) * LOG2_E

    def attend(keys, values, positions):
        scores = dot_nt(query_ref[...], keys)
        scores = jnp.where(positions <= limit_ref[...], scores, LOW)
        old_peak = peak_ref[...]
        peak = jnp.maximum(old_peak, jnp.max(scores, axis=1, keepdims=True))
        shrink = jnp.exp2((old_peak - peak) * slope)
        weights = jnp.exp2((scores - peak) * slope).astype(jnp.bfloat16)
        peak_ref[...] = peak
        wide = jnp.concatenate([values, jnp.ones(values.shape, jnp.bfloat16)], axis=1)
        mixed_ref[...] = mixed_ref[...] * shrink + dot(weights, wide)

    def pool_unit(place, unit):
        rows = pl.ds(unit * half, half)
        keys, values = [], []
        for token in range(PAGE):
            for which in range(4):
                block = place * 4 + which
                table = 0 if shared else block
                start = token * width
                raw = pool_all[block, rows, start : start + dim].astype(jnp.float32)
                keys.append(
                    turn(raw, cos_ref[table, rows, :], sin_ref[table, rows, :]).astype(jnp.bfloat16)
                )
                values.append(pool_all[block, rows, start + dim : start + width])
        keys = jnp.concatenate(keys, axis=0)
        values = jnp.concatenate(values, axis=0)
        attend(keys, values, key_pos[place * 2 + unit])
        choose = jnp.where(page_pos[place * 2 + unit] == wanted_ref[...], 1.0, 0.0)
        choose = choose.astype(jnp.bfloat16)
        size = 4 * half
        for token in range(PAGE):
            part = slice(token * size, (token + 1) * size)
            both = jnp.concatenate([keys[part], values[part]], axis=1)
            page_acc[:, token * width : (token + 1) * width] += dot(choose, both)

    def fresh_unit(place):
        both = jnp.concatenate(
            [fresh_all[place * 4 + which].astype(jnp.float32) for which in range(4)], axis=0
        ).astype(jnp.bfloat16)
        positions = fresh_pos[place]
        attend(both[:, :dim], both[:, dim:], positions)
        for token in range(PAGE):
            choose = jnp.where(positions == wanted_ref[...] * PAGE + token, 1.0, 0.0)
            fresh_acc[token] += dot(choose.astype(jnp.bfloat16), both)

    def compute(step, needed, work):
        @pl.loop(0, 2)
        def _(way):
            place = jnp.where(way == 0, at - step, at + step)
            exists = jnp.where(
                way == 0, at - step >= 0, (at + step < length) & (step > 0)
            )

            @pl.when(exists)
            def _():
                for part in needed:
                    arrive(part, place * 4 + twin_inner)
                    arrive(part, place * 4 + across_twin)
                work(place)

    own_copy.wait()

    @pl.loop(0, length)
    def _(step):
        line(step + 1, 0, begin, True)
        crossed(step, 0, begin, True)
        compute(step, (0,), lambda place: pool_unit(place, 0))
        line(step + 1, fresh, begin, True)
        crossed(step, fresh, begin, True)
        compute(step, (fresh,), fresh_unit)
        for part in range(2, last + 1):
            line(step + 1, part, begin, True)
            if part != last:
                crossed(step, part, begin, True)
        compute(step, tuple(range(2, last + 1)), lambda place: pool_unit(place, 1))

    for head in range(GROUP):
        rows = slice(head * sel, (head + 1) * sel)
        attended[:, head * dim : (head + 1) * dim] = (
            mixed_ref[rows, :dim] / mixed_ref[rows, dim:]
        ).astype(jnp.bfloat16)
    for token in range(PAGE):
        columns = slice(token * width, (token + 1) * width)
        pages[:, columns] = jnp.where(
            keep_ref[token] > 0.5, page_acc[:, columns], fresh_acc[token]
        ).astype(jnp.bfloat16)

    send_pool(settle)
    send_fresh(settle)
    pass_across_first(settle)

    @pl.loop(0, length)
    def _(step):
        for part in range(last + 1):
            line(step + 1, part, settle, False)
        for part in lined:
            crossed(step, part, settle, False)


def shards(
    pool_kv, pool_slot, passage_order, passage_start, recompute_pos, page_table, fresh_q, fresh_kv
):
    count = lax.axis_size("seq")
    page_count = pool_kv.shape[0]
    sel, width = fresh_kv.shape
    dim = width // 2
    length = count // 4
    half, lined_pool, _ = pool_parts(page_count, count)
    parts = len(lined_pool) + 2
    tables = 1 if page_count % count == 0 else count
    bf16, f32, i32 = jnp.bfloat16, jnp.float32, jnp.int32
    frequency = ROPE_BASE ** (-(jnp.arange(dim // 2, dtype=f32) * (2.0 / dim)))
    frequency = jnp.concatenate([frequency, frequency])[None, :]
    held = [
        fresh_kv,
        fresh_q,
        pool_slot[None, :],
        passage_order[None, :],
        passage_start[None, :],
        recompute_pos,
        page_table.reshape(-1, 128),
        frequency,
    ]
    queries = sel * GROUP
    return pl.pallas_call(
        lambda *refs: kernel(count, *refs),
        out_shape=(
            jax.ShapeDtypeStruct((sel, GROUP * dim), bf16),
            jax.ShapeDtypeStruct(pool_kv.shape, bf16),
        ),
        in_specs=[pl.BlockSpec(memory_space=pl.ANY)] * (1 + len(held)),
        out_specs=(
            pl.BlockSpec(memory_space=pltpu.VMEM),
            pl.BlockSpec(memory_space=pltpu.VMEM),
        ),
        scratch_shapes=[
            pltpu.VMEM((count, *pool_kv.shape), bf16),
            pltpu.VMEM((count, sel, width), bf16),
            *(pltpu.VMEM(one.shape, one.dtype) for one in held),
            pltpu.VMEM((queries, dim), bf16),
            pltpu.VMEM((queries, 1), i32),
            pltpu.VMEM((tables, page_count, dim), f32),
            pltpu.VMEM((tables, page_count, dim), f32),
            pltpu.VMEM((2 * length, 1, PAGE * 4 * half), i32),
            pltpu.VMEM((2 * length, 1, 4 * half), i32),
            pltpu.VMEM((length, 1, 4 * sel), i32),
            pltpu.VMEM((page_count, 1), i32),
            pltpu.VMEM((PAGE, page_count, 1), f32),
            pltpu.VMEM((queries, 1), f32),
            pltpu.VMEM((queries, width), f32),
            pltpu.VMEM((page_count, PAGE * width), f32),
            pltpu.VMEM((PAGE, page_count, width), f32),
            pltpu.SemaphoreType.DMA((4, parts, count)),
            pltpu.SemaphoreType.DMA((parts, count)),
            pltpu.SemaphoreType.DMA((len(held) + 1,)),
        ],
        compiler_params=pltpu.CompilerParams(collective_id=0, has_side_effects=True),
    )(pool_kv, *held)


def solution(mesh):
    placed = (
        P(("groups", "seq"), None),
        P("groups"),
        P("groups"),
        P("groups"),
        P("groups", None),
        P("groups"),
        P(("groups", "seq"), None),
        P(("groups", "seq"), None),
    )
    return jax.shard_map(
        shards,
        mesh=mesh,
        in_specs=placed,
        out_specs=(P(("groups", "seq"), None), P(("groups", "seq"), None)),
        check_vma=False,
    )
```
